128 devices in a mesh: shard: 32 (over y, z_hi, x), tensor: 4 (over z_lo, core).
Axes of the slice: x: 4, y: 4, z: 4 (z_hi: 2, z_lo: 2; z = z_hi * 2 + z_lo), core: 2. Of those that a mesh axis runs over, the one named last changes fastest.
Arguments:
- acts: bfloat16 [32768, 768], P('shard', 'tensor')
- out_grads: bfloat16 [2, 32768, 768], P(None, 'shard', 'tensor')
- sampled_rows: int32 [2, 262144], P(None, 'shard'), may hold values from 0 to 1023
- proj_grad: float32 [768, 768], P(('shard', 'tensor')), may hold values from -600 to 600
- proj_momentum: float32 [768, 768], P(('shard', 'tensor')), may hold values from -6 to 6
- embed_grad: float32 [49152, 768], P(('shard', 'tensor')), may hold values from -36 to 36
- embed_momentum: float32 [49152, 768], P(('shard', 'tensor')), may hold values from -6 to 6
- token_counts: int32 [49152], P(('shard', 'tensor')), may hold values from 0 to 99
Outputs:
- proj_momentum_new: float32 [768, 768], P(('shard', 'tensor'))
- embed_momentum_new: float32 [49152, 768], P(('shard', 'tensor'))
The draws below stay inside these ranges and needn't reach their ends.
Inputs may be any that keep to these rules, and one draw needn't show every extreme that they name: `sampled_rows`: entry j of a row picks token (j // 8192) * 1024 + value, one of the 1024 tokens of its index of shard; repeats are allowed.
All inputs are finite; a program needn't handle non-finite values.
Results may differ from the reference program's by a relative error of at most 0.0003.
Values may be sent and summed in bfloat16 or wider, within the bound.
No kernel may reach another device: no remote copies, remote signals or barrier semaphores. Data moves between devices by JAX's collectives and lax.ppermute only.
A program may use at most 128 MiB of HBM per device.

```python
import math
import jax
import jax.numpy as jnp
from jax import lax

D = 768
VOCAB = 49152
TOK_DEV = 1024
SAMPLE = 2048
NS_ITERS = 3
TOKENS = 32768
SAMPLES = 262144
N_SHARD = 32
N_TENSOR = 4


def scaled_features(key, layers, rows, width):
    key_base, key_rows, key_cols = jax.random.split(key, 3)
    base = jax.random.normal(key_base, (layers, rows, width), jnp.float32)
    lowest = 0.3
    uppermost = 3.0
    spread = math.log(uppermost / lowest)
    row_scale = lowest * jnp.exp(spread * jax.random.uniform(key_rows, (layers, rows, 1), jnp.float32))
    col_scale = lowest * jnp.exp(spread * jax.random.uniform(key_cols, (layers, 1, width), jnp.float32))
    rising = jnp.sqrt(1.0 + 2.0 * jnp.arange(rows, dtype=jnp.float32) / rows)[None, :, None]
    return base * row_scale * col_scale * rising


def draw_acts(key, part):
    return scaled_features(jax.random.fold_in(key, 11), 1, TOKENS, D)[0].astype(jnp.bfloat16)


def draw_out_grads(key, part):
    return scaled_features(jax.random.fold_in(key, 23), 2, TOKENS, D).astype(jnp.bfloat16)


def draw_token_counts(key, part):
    places = jnp.arange(VOCAB, dtype=jnp.int32)
    ceiling = 100 - 68 * places // VOCAB
    raw = jax.random.randint(jax.random.fold_in(key, 37), (VOCAB,), 0, 1048576, dtype=jnp.int32)
    counts = raw * ceiling // 1048576
    counts = jnp.where(places == 0, 99, jnp.where(places == VOCAB - 1, 0, counts))
    return counts.astype(jnp.int32)


def plant(drawn, own_key, smallest, largest):
    place = [jax.random.randint(jax.random.fold_in(own_key, axis), (), 0, length) for axis, length in enumerate(drawn.shape)]
    main_axis = drawn.shape.index(max(drawn.shape))
    next_to = place[:main_axis] + [(place[main_axis] + 1) % drawn.shape[main_axis]] + place[main_axis + 1:]
    return drawn.at[tuple(place)].set(smallest).at[tuple(next_to)].set(largest)


def shard_levels(key, extent, shards, smallest, largest):
    def one(position, parts):
        draws = jax.random.uniform(jax.random.fold_in(jax.random.fold_in(key, 6), position), (parts,), jnp.float32, smallest / len(shards), largest / len(shards))
        return jnp.repeat(jnp.exp(draws), extent[position] // parts).reshape((-1,) + (1,) * (len(extent) - position - 1))

    factor_of = one(*shards[0])
    for cut in shards[1:]:
        factor_of = factor_of * one(*cut)
    return factor_of


def normal_values(own_key, extent, deviation, most, pieces=(), kind=jnp.bfloat16):
    factor_of = shard_levels(own_key, extent, pieces, -0.22, 0.18) if pieces else 1.0
    drawn = jax.random.normal(own_key, extent, jnp.float32) * deviation * factor_of
    return jnp.minimum(jnp.maximum(drawn, -most), most).astype(kind)


def setup_inputs(seed: int = 0) -> dict:
    key_of = jax.random.split(jax.random.key(seed), 9)
    acts = draw_acts(jax.random.fold_in(key_of[8], 71), 0)
    out_grads = draw_out_grads(jax.random.fold_in(key_of[8], 71), 0)
    sampled_rows = plant(jax.random.randint(key_of[2], (2, SAMPLES), 0, TOK_DEV), jax.random.fold_in(key_of[2], 1), 0, TOK_DEV - 1).astype(jnp.int32)
    proj_grad = normal_values(key_of[3], (D, D), 100.0, 600.0, ((0, 128),), jnp.float32)
    proj_momentum = normal_values(key_of[4], (D, D), 1.0, 6.0, ((0, 128),), jnp.float32)
    embed_grad = normal_values(key_of[5], (VOCAB, D), 6.0, 36.0, ((0, 128),), jnp.float32)
    embed_momentum = normal_values(key_of[6], (VOCAB, D), 1.0, 6.0, ((0, 128),), jnp.float32)
    token_counts = draw_token_counts(jax.random.fold_in(key_of[8], 71), 0)
    return dict(acts=acts, out_grads=out_grads, sampled_rows=sampled_rows, proj_grad=proj_grad, proj_momentum=proj_momentum, embed_grad=embed_grad, embed_momentum=embed_momentum, token_counts=token_counts)


momentum_decay = 0.9
damping_root = 0.5
count_scale = 64.0
highest = lax.Precision.HIGHEST

def newton_inverse(factor, trace, shift):
    width = factor.shape[0]
    identity = jnp.eye(width, dtype=jnp.float32)
    norm_sq = jnp.sum(factor * factor) + 2.0 * shift * trace + width * shift * shift
    start_scale = 1.0 / jnp.sqrt(norm_sq)
    damped = factor + shift * identity
    iterate = 2.0 * start_scale * identity - start_scale * start_scale * damped
    for iteration in range(NS_ITERS - 1):
        product = jnp.dot(damped, iterate, precision=highest)
        iterate = 2.0 * iterate - jnp.dot(product, iterate, precision=highest)
    return iterate

def reference(acts, out_grads, sampled_rows, proj_grad, proj_momentum, embed_grad, embed_momentum, token_counts):
    devices_all = N_SHARD * N_TENSOR
    sample_total = SAMPLE * devices_all

    def accumulate(device, carry):
        factors, traces = carry
        device = jnp.asarray(device).astype(jnp.int32)
        chosen = lax.dynamic_slice_in_dim(sampled_rows, device * SAMPLE, SAMPLE, 1).astype(jnp.int32)
        offset = (device // N_TENSOR * TOK_DEV).astype(jnp.int32)
        stacked = jnp.stack([acts[offset + chosen[0]], out_grads[0][offset + chosen[0]], out_grads[1][offset + chosen[1]]]).astype(jnp.float32)
        factors = factors + jnp.einsum('fsd,fse->fde', stacked, stacked, precision=highest)
        traces = traces + lax.optimization_barrier(jnp.sum(stacked * stacked, axis=(1, 2)))
        return (factors, traces)
    start = (jnp.zeros((3, D, D), jnp.float32), jnp.zeros((3,), jnp.float32))
    factors, traces = lax.fori_loop(0, devices_all, accumulate, start)
    factors = factors / sample_total
    traces = traces / sample_total
    count_total = jnp.sum(token_counts.astype(jnp.float32))
    ratio = jnp.sqrt(traces[0] / traces[1])
    embed_ratio = jnp.sqrt(count_total / count_scale / VOCAB / (traces[2] / D))
    a_inverse = newton_inverse(factors[0], traces[0], damping_root * ratio)
    g_inverse = newton_inverse(factors[1], traces[1], damping_root / ratio)
    e_inverse = newton_inverse(factors[2], traces[2], damping_root / embed_ratio)
    mixed = jnp.dot(proj_grad, g_inverse, precision=highest)
    update = jnp.dot(a_inverse, mixed, precision=highest)
    row_scale = token_counts.astype(jnp.float32) / count_scale + damping_root * embed_ratio
    embed_update = jnp.dot(embed_grad, e_inverse, precision=highest) / row_scale[:, None]
    return (momentum_decay * proj_momentum + update, momentum_decay * embed_momentum + embed_update)
```

```python
import jax
import jax.numpy as jnp
from jax import lax
from jax.experimental import pallas as pl
from jax.experimental.pallas import tpu as pltpu
from jax.sharding import Mesh, PartitionSpec as P

D = 768
VOCAB = 49152
SAMPLES = 262144
TERMS = 8
BLK = 128
NB = D // BLK
momentum_decay = 0.9
damping_root = 0.5
count_scale = 64.0
f32 = jnp.float32
bf16 = jnp.bfloat16
CHIPS = ("y", "zhi", "x", "zlo")
G_ROWS = 36
F_ROWS = 64
ROWS = F_ROWS + 2 * G_ROWS + 8

PAIRS = [(i, i) for i in range(NB)] + [(i, j) for i in range(NB) for j in range(i + 1, NB)]
PER = len(PAIRS)
VMEM = pl.BlockSpec(memory_space=pltpu.VMEM)
SMEM = pl.BlockSpec(memory_space=pltpu.SMEM)


def pieces(v, n):
    out = []
    for _ in range(n):
        p = v.astype(bf16)
        out.append(p)
        v = v - p.astype(f32)
    return out


def factor_kernel(meta, samples, x, out):
    core = meta[0]
    first = meta[1]
    tokens = x.shape[1]
    token_ids = lax.broadcasted_iota(jnp.int32, (tokens, BLK), 0) + first
    counts = []
    for k in range(2):

        def count(step, acc):
            row = samples[k : k + 1, pl.ds(pl.multiple_of(step * BLK, BLK), BLK)]
            return acc + jnp.where(token_ids == row, 1.0, 0.0)

        acc = lax.fori_loop(0, samples.shape[1] // BLK, count, jnp.zeros((tokens, BLK), f32), unroll=4)
        counts.append(jnp.sum(acc, axis=1, keepdims=True))
    for m in range(3):
        xs = x[m]
        hi, lo = pieces(xs.astype(f32) * counts[m // 2], 2)
        left = jnp.concatenate([hi, lo], axis=0)
        right = jnp.concatenate([xs, xs], axis=0)
        for i in range(NB):
            block_row = lax.dot_general(
                left[:, i * BLK : (i + 1) * BLK],
                right[:, i * BLK :],
                (((0,), (0,)), ((), ())),
                preferred_element_type=f32,
            ) * (1.0 / SAMPLES)
            for j in range(i, NB):
                b = m * PER + PAIRS.index((i, j))
                block = block_row[:, (j - i) * BLK : (j - i + 1) * BLK].astype(bf16)
                for half in range(2):
                    h = 2 * b + half
                    out[(h // 64 + core) % 2, h % 64] = block[half * 64 : (half + 1) * 64]
    for h in (126, 127):
        out[(h // 64 + core) % 2, h % 64] = jnp.zeros((64, BLK), bf16)


def pack_kernel(meta, parts, grad, counts, out):
    h = meta[0]
    total = jnp.sum(parts[...].astype(f32), axis=0)
    rows = lax.broadcasted_iota(jnp.int32, (64, BLK), 0) + (h % 2) * 64
    lanes = lax.broadcasted_iota(jnp.int32, (64, BLK), 1)
    is_diag = (h // 2) % PER < NB

    def full_sum(v):
        return jnp.sum(jnp.sum(v, axis=1, keepdims=True), axis=0, keepdims=True)

    norm = full_sum(total * total) * jnp.where(is_diag, 1.0, 2.0)
    trace = full_sum(jnp.where((rows == lanes) & is_diag, total, 0.0))
    count = full_sum(counts[...].astype(f32))
    scalars = pieces(norm, 3) + pieces(trace, 3) + pieces(count, 2)
    row8 = lax.broadcasted_iota(jnp.int32, (8, BLK), 0)
    tail = jnp.zeros((8, BLK), f32)
    for r, s in enumerate(scalars):
        tail = jnp.where(row8 == r, s.astype(f32), tail)
    g_hi, g_lo = pieces(grad[...], 2)
    payload = jnp.concatenate(
        [total.astype(bf16).astype(f32), g_hi.astype(f32), g_lo.astype(f32), tail], axis=0
    ).astype(bf16)
    out[...] = jnp.broadcast_to(payload[None], out.shape)


def apply_rows(v, factor, keep, scale, n):
    rows = v.shape[0]
    w = v
    for _ in range(TERMS - 1):
        stacked = jnp.concatenate(pieces(w, n), axis=0)
        product = jnp.dot(stacked, factor[...], preferred_element_type=f32)
        total = product[:rows]
        for p in range(1, n):
            total = total + product[p * rows : (p + 1) * rows]
        w = v + keep * w - scale * total
    return w


def update_kernel(meta, mine, theirs, g_hi, g_lo, embed, embed_mom, counts, proj_mom, out_proj, out_embed, every, factors):
    core = meta[0]
    first_row = meta[1]
    every[core] = mine[...]
    every[1 - core] = theirs[...]
    norms, traces, count_total = [], [], jnp.zeros((1, 1), f32)
    for m in range(3):
        acc = jnp.zeros((16, BLK), f32)
        for h in range(42 * m, 42 * m + 42 + (2 if m == 2 else 0)):
            acc = acc + every[h // 64, h % 64, ROWS - 16 : ROWS, :].astype(f32)
        acc = acc[8:, 0:1]
        norms.append(acc[0:1] + acc[1:2] + acc[2:3])
        traces.append(acc[3:4] + acc[4:5] + acc[5:6])
        count_total = count_total + acc[6:7] + acc[7:8]
    ratio = jnp.sqrt(traces[0] / traces[1])
    embed_ratio = jnp.sqrt(count_total / count_scale / VOCAB / (traces[2] / D))
    shifts = [damping_root * ratio, damping_root / ratio, damping_root / embed_ratio]
    scales = [
        1.0 / jnp.sqrt(norms[m] + 2.0 * shifts[m] * traces[m] + D * shifts[m] * shifts[m])
        for m in range(3)
    ]
    keeps = [1.0 - scales[m] * shifts[m] for m in range(3)]
    for m in range(3):
        for p, (i, j) in enumerate(PAIRS):
            h = 2 * (m * PER + p)
            block = jnp.concatenate(
                [every[h // 64, h % 64, :F_ROWS, :], every[h // 64, (h + 1) % 64, :F_ROWS, :]], axis=0
            )
            factors[m, i * BLK : (i + 1) * BLK, j * BLK : (j + 1) * BLK] = block
            if i != j:
                factors[m, j * BLK : (j + 1) * BLK, i * BLK : (i + 1) * BLK] = block.T
    rows = lax.broadcasted_iota(jnp.int32, (8, D), 0) + first_row
    eye_rows = jnp.where(lax.broadcasted_iota(jnp.int32, (8, D), 1) == rows, 1.0, 0.0)
    left = apply_rows(eye_rows, factors.at[0], keeps[0], scales[0], 3) * scales[0]
    split = pieces(left, 3)
    big = jnp.dot(jnp.concatenate(split, axis=0), g_hi[...], preferred_element_type=f32)
    small = jnp.dot(jnp.concatenate(split[:2], axis=0), g_lo[...], preferred_element_type=f32)
    mixed = big[:8] + big[8:16] + big[16:] + small[:8] + small[8:]
    update = apply_rows(mixed, factors.at[1], keeps[1], scales[1], 3) * scales[1]
    out_proj[...] = momentum_decay * proj_mom[...] + update[:6]
    result = apply_rows(embed[...], factors.at[2], keeps[2], scales[2], 2) * scales[2]
    row_scale = counts[...].astype(f32) / count_scale + damping_root * embed_ratio
    out_embed[...] = momentum_decay * embed_mom[...] + result / row_scale


def per_device(acts, out_grads, sampled_rows, proj_grad, proj_momentum, embed_grad, embed_momentum, token_counts):
    core = lax.axis_index("core")
    chip = lax.axis_index(CHIPS)
    tensor = lax.axis_index(("zlo", "core"))
    tokens = acts.shape[0] // 4
    params = pltpu.CompilerParams(vmem_limit_bytes=56 * 1024 * 1024)
    flat = jnp.stack([acts, out_grads[0], out_grads[1]])
    x = lax.all_to_all(flat, ("zlo", "core"), split_axis=1, concat_axis=2, tiled=True)
    halves = pl.pallas_call(
        factor_kernel,
        out_shape=jax.ShapeDtypeStruct((2, 64, 64, BLK), bf16),
        in_specs=[SMEM, VMEM, VMEM],
        out_specs=VMEM,
        compiler_params=params,
        name="factor",
    )(jnp.stack([core, tensor * tokens]).astype(jnp.int32), sampled_rows, x)
    swap = [(0, 1), (1, 0)]
    pair = halves[0].astype(f32) + lax.ppermute(halves[1], "core", swap).astype(f32)
    parts = lax.all_to_all(pair.astype(bf16), CHIPS, split_axis=0, concat_axis=0, tiled=True)
    payload = pl.pallas_call(
        pack_kernel,
        out_shape=jax.ShapeDtypeStruct((64, ROWS, BLK), bf16),
        in_specs=[SMEM, VMEM, VMEM, VMEM],
        out_specs=VMEM,
        compiler_params=params,
        name="pack",
    )(
        (core * 64 + chip)[None].astype(jnp.int32),
        parts,
        proj_grad.reshape(G_ROWS, BLK),
        token_counts.reshape(3, BLK),
    )
    mine = lax.all_to_all(payload, CHIPS, split_axis=0, concat_axis=0, tiled=True)
    theirs = lax.ppermute(mine, "core", swap)
    g_mine = mine[:, F_ROWS : F_ROWS + 2 * G_ROWS]
    g_theirs = theirs[:, F_ROWS : F_ROWS + 2 * G_ROWS]
    even = jnp.where(core == 0, g_mine, g_theirs)
    odd = jnp.where(core == 0, g_theirs, g_mine)
    g_all = jnp.stack([even, odd], axis=1)
    g_hi = g_all[:, :, :G_ROWS].reshape(D, D)
    g_lo = g_all[:, :, G_ROWS:].reshape(D, D)
    first_row = (chip * 2 + core) * 6
    return pl.pallas_call(
        update_kernel,
        out_shape=(
            jax.ShapeDtypeStruct(proj_momentum.shape, f32),
            jax.ShapeDtypeStruct(embed_momentum.shape, f32),
        ),
        in_specs=[SMEM] + [VMEM] * 8,
        out_specs=(VMEM, VMEM),
        scratch_shapes=[pltpu.VMEM((2, 64, ROWS, BLK), bf16), pltpu.VMEM((3, D, D), bf16)],
        compiler_params=params,
        name="update",
    )(
        jnp.stack([core, first_row]).astype(jnp.int32),
        mine,
        theirs,
        g_hi,
        g_lo,
        embed_grad,
        embed_momentum,
        token_counts[:, None],
        proj_momentum,
    )


def solution(mesh):
    fine = Mesh(mesh.devices.reshape(4, 2, 4, 2, 2), ("y", "zhi", "x", "zlo", "core"))
    shard = ("y", "zhi", "x")
    tensor = ("zlo", "core")
    rows = P(shard + tensor, None)
    return jax.shard_map(
        per_device,
        mesh=fine,
        in_specs=(
            P(shard, tensor),
            P(None, shard, tensor),
            P(None, shard),
            rows,
            rows,
            rows,
            rows,
            P(shard + tensor),
        ),
        out_specs=(rows, rows),
        check_vma=False,
    )
```
